32 devices in a mesh: view: 2 (over core), gz: 8 (over z, y), gy: 2 (over x).
Axes of the slice: x: 2, y: 2, z: 4, core: 2. Of those that a mesh axis runs over, the one named last changes fastest.
Arguments:
- observed: float32 [2, 512, 32, 256], P('view', 'gz', 'gy'), may hold values from 0.5 to 4
- start: float32 [512, 32, 256], P('gz', 'gy'), may hold values from 0.5 to 2
- spread_z: float32 [2, 31], P('view'), may hold values from 0.05 to 1
- spread_y: float32 [2, 7], P('view'), may hold values from 0.1 to 1
- spread_x: float32 [2, 7], P('view'), may hold values from 0.1 to 1
Outputs:
- estimate: float32 [512, 32, 256], P('gz', 'gy')
The draws below stay inside these ranges and needn't reach their ends.
All inputs are finite; a program needn't handle non-finite values.
Results may differ from the reference program's by a relative error of at most 0.0001.
Values sent between devices are 32-bit elements; how exact they have to be, the bound alone decides.
A program may use at most 64 MiB of HBM per device.

```python
import math
import jax
import jax.numpy as jnp
from jax import lax

NX = 256
KZ = 31
KY = 7
KX = 7
ITERS = 2
NZ = 512
NY = 32
N_VIEW = 2


def level_of(own_key, extent, pieces, least, top_value):
    loudness = 1.0
    for axis_at, shards_of in pieces:
        draws = jax.random.uniform(jax.random.fold_in(jax.random.fold_in(own_key, 6), axis_at), (shards_of,), jnp.float32, least / len(pieces), top_value / len(pieces))
        loudness = loudness * jnp.repeat(jnp.exp(draws), extent[axis_at] // shards_of).reshape((-1,) + (1,) * (len(extent) - 1 - axis_at))
    return loudness


def setup_inputs(seed: int = 0) -> dict:
    key_of = jax.random.split(jax.random.key(seed), 6)
    observed = jnp.clip(jnp.exp(math.log(4.0) - 2.0794415 * jax.random.uniform(key_of[0], (N_VIEW, NZ, NY, NX), jnp.float32) ** level_of(key_of[0], (N_VIEW, NZ, NY, NX), ((0, 2), (1, 8), (2, 2)), -0.2, 0.2)), 0.5, 4.0)
    start = jnp.clip(jnp.exp(math.log(2.0) - 1.3862944 * jax.random.uniform(key_of[1], (NZ, NY, NX), jnp.float32) ** level_of(key_of[1], (NZ, NY, NX), ((0, 8), (1, 2)), -0.2, 0.2)), 0.5, 2.0)
    spread_z = jnp.clip(jnp.exp(math.log(1.0) - 2.9957323 * jax.random.uniform(key_of[2], (N_VIEW, KZ), jnp.float32) ** level_of(key_of[2], (N_VIEW, KZ), ((0, 2),), -0.2, 0.2)), 0.05, 1.0)
    spread_y = jnp.clip(jnp.exp(math.log(1.0) - 2.3025851 * jax.random.uniform(key_of[3], (N_VIEW, KY), jnp.float32) ** level_of(key_of[3], (N_VIEW, KY), ((0, 2),), -0.2, 0.2)), 0.1, 1.0)
    spread_x = jnp.clip(jnp.exp(math.log(1.0) - 2.3025851 * jax.random.uniform(key_of[4], (N_VIEW, KX), jnp.float32) ** level_of(key_of[4], (N_VIEW, KX), ((0, 2),), -0.2, 0.2)), 0.1, 1.0)
    return dict(observed=observed, start=start, spread_z=spread_z, spread_y=spread_y, spread_x=spread_x)


def correlate(field, weights, along, margin):
    padding = [(0, 0), (0, 0), (0, 0)]
    padding[along] = (margin, margin)
    padded = jnp.pad(field, padding)
    taps = weights.shape[0]
    length = padded.shape[along] - taps + 1
    total = weights[0] * lax.slice_in_dim(padded, 0, length, 1, along)
    for offset in range(1, taps):
        total = total + weights[offset] * lax.slice_in_dim(padded, offset, offset + length, 1, along)
    return total


def blur(field, weight_z, weight_y, weight_x):
    field = correlate(field, weight_z, 0, KZ // 2)
    field = correlate(field, weight_y, 1, KY // 2)
    return correlate(field, weight_x, 2, KX // 2)


def normalized(profile):
    return profile / jnp.sum(profile)


def reference(observed, start, spread_z, spread_y, spread_x):
    estimate = start
    for sweep in range(ITERS):
        summed = jnp.zeros_like(start)
        for which_view in range(2):
            weight_z = normalized(spread_z[which_view])
            weight_y = normalized(spread_y[which_view])
            weight_x = normalized(spread_x[which_view])
            blurred = blur(estimate, weight_z, weight_y, weight_x)
            quotient = observed[which_view] / blurred
            summed = summed + blur(quotient, weight_z[::-1], weight_y[::-1], weight_x[::-1])
        estimate = estimate * (0.5 * summed)
    return estimate
```

```python
import functools

import jax
import jax.numpy as jnp
from jax import lax
from jax.experimental import pallas as pl
from jax.experimental.pallas import tpu as pltpu
from jax.sharding import PartitionSpec as P

ITERS = 2
MESH = pl.DeviceIdType.MESH
F32 = jnp.float32
BF16 = jnp.bfloat16


def split(x):
    high = x.astype(BF16)
    return high, (x - high.astype(F32)).astype(BF16)


def kernel(dims, obs_hbm, start_hbm, sz_ref, sy_ref, sx_ref, out_hbm,
           stage, obs_z, obs_t, mine, theirs, wf, wb, tx, zbuf, ybuf, qbuf,
           ebuf, cbuf, rybuf, rzbuf, lsem, ssem, rsem, xssem, xrsem):
    NH, NY, NX, HZ, KZ, KY, KX, S, G = dims
    my, mz, mx = KY // 2, KZ // 2, KX // 2
    NE, NR = NH + 2 * HZ, NY + 2 * my
    v = lax.axis_index("view")
    gy = lax.axis_index("gy")
    s = 2 * lax.axis_index("gz") + v
    up_z, dn_z = s < S - 1, s > 0
    up_y, dn_y = gy < G - 1, gy > 0

    def zdev(t):
        t = lax.rem(t + S, S)
        return {"view": lax.rem(t, 2), "gz": t // 2}

    def ydev(t):
        return {"gy": lax.rem(t + G, G)}

    zto = (zdev(s + 1), zdev(s - 1))
    yto = (ydev(gy + 1), ydev(gy - 1))
    partner = {"view": 1 - v}
    zhas, yhas = (up_z, dn_z), (up_y, dn_y)
    zfrom, yfrom = (dn_z, up_z), (dn_y, up_y)

    load_start = pltpu.make_async_copy(start_hbm.at[pl.ds(v * NH, NH)], stage.at[0], lsem.at[0])
    load_start.start()
    load_obs = pltpu.make_async_copy(obs_hbm.at[0, pl.ds(v * NH, NH)], obs_z.at[v], lsem.at[1])
    load_obs.start()

    barrier = pltpu.get_barrier_semaphore()
    for has, to in ((up_z, zto[0]), (dn_z, zto[1]), (up_y, yto[0]), (dn_y, yto[1])):
        @pl.when(has)
        def _(to=to):
            pl.semaphore_signal(barrier, inc=1, device_id=to, device_id_type=MESH)

    mine[...] = jnp.zeros_like(mine)
    for row, (ref, taps) in enumerate(((sz_ref, KZ), (sy_ref, KY), (sx_ref, KX))):
        raw = ref[...]
        mine[row:row + 1, 0:taps] = raw / jnp.sum(raw, axis=1, keepdims=True)
    for it in range(ITERS):
        for d in range(2):
            @pl.when(jnp.logical_not(zfrom[d]))
            def _(it=it, d=d):
                z0 = (0, HZ + NH)[d]
                ebuf[it, :, z0:z0 + HZ, :] = jnp.zeros((NR, HZ, NX), F32)

            @pl.when(jnp.logical_not(yfrom[d]))
            def _(it=it, d=d):
                r0 = (0, my + NY)[d]
                ebuf[it, r0:r0 + my] = jnp.zeros((my, NE, NX), F32)

    load_start.wait()
    ebuf[0, my:my + NY, HZ:HZ + NH, :] = jnp.transpose(stage[0], (1, 0, 2))

    peers = sum(has.astype(jnp.int32) for has in (up_z, dn_z, up_y, dn_y))
    pl.semaphore_wait(barrier, peers)

    def copy(phase, m, src, dst, to):
        return pltpu.make_async_remote_copy(
            src_ref=src, dst_ref=dst, send_sem=ssem.at[phase, m], recv_sem=rsem.at[phase, m],
            device_id=to, device_id_type=MESH)

    ROWS = ((my, my), (my + 2 * my - my, NY - 2 * my), (NY, my))
    ZED = ((HZ, NH), (0, HZ), (HZ + NH, HZ))

    def gather_z(it):
        e = ebuf.at[it]
        out = []
        for d in range(2):
            src0, dst0 = ((NH, 0), (HZ, HZ + NH))[d]
            for p, (r0, n) in enumerate(ROWS):
                out.append(copy(2 * it, 3 * d + p, e.at[pl.ds(r0, n), pl.ds(src0, HZ)],
                                e.at[pl.ds(r0, n), pl.ds(dst0, HZ)], zto[d]))
        return out

    def gather_y(it):
        e = ebuf.at[it]
        out = []
        for d in range(2):
            src0, dst0 = ((NY, 0), (my, my + NY))[d]
            for p, (z0, n) in enumerate(ZED):
                out.append(copy(2 * it, 6 + 3 * d + p, e.at[pl.ds(src0, my), pl.ds(z0, n)],
                                e.at[pl.ds(dst0, my), pl.ds(z0, n)], yto[d]))
        return out

    def when(cond, fn):
        @pl.when(cond)
        def _():
            fn()

    def both(a, b):
        return jnp.logical_and(a, b)

    zed_has = (None, dn_z, up_z)

    def gather_begin(it):
        gz_, gy_ = gather_z(it), gather_y(it)
        for p in (0, 2, 1):
            for d in range(2):
                when(zhas[d], gz_[3 * d + p].start)
        for d in range(2):
            when(yhas[d], gy_[3 * d].start)

    def gather_end(it):
        gz_, gy_ = gather_z(it), gather_y(it)
        for d in range(2):
            for p, dy in ((0, 1), (2, 0)):
                when(zfrom[d], gz_[3 * d + p].wait_recv)
                when(both(zfrom[d], yhas[dy]), gy_[3 * dy + 1 + d].start)
        for d in range(2):
            when(zfrom[d], gz_[3 * d + 1].wait_recv)
            when(yfrom[d], gy_[3 * d].wait_recv)
            for q in range(2):
                when(both(zed_has[1 + q], yfrom[d]), gy_[3 * d + 1 + q].wait_recv)
        for d in range(2):
            for p in range(3):
                when(zhas[d], gz_[3 * d + p].wait_send)
            when(yhas[d], gy_[3 * d].wait_send)
            for q in range(2):
                when(both(zed_has[1 + q], yhas[d]), gy_[3 * d + 1 + q].wait_send)

    def scatter(it):
        c, ry, rz = cbuf.at[it], rybuf.at[it], rzbuf.at[it]
        ph = 2 * it + 1
        sy_, sz_ = [], []
        for d in range(2):
            src0 = (my + NY, 0)[d]
            for p, (z0, n) in enumerate(ZED):
                sy_.append(copy(ph, 6 + 3 * d + p, c.at[pl.ds(src0, my), pl.ds(z0, n)],
                                ry.at[d, :, pl.ds(z0, n)], yto[d]))
            src0 = (HZ + NH, 0)[d]
            for p, (r0, n) in enumerate(ROWS):
                sz_.append(copy(ph, 3 * d + p, c.at[pl.ds(r0, n), pl.ds(src0, HZ)],
                                rz.at[d, pl.ds(r0 - my, n)], zto[d]))
        for q in range(2):
            for d in range(2):
                when(both(zed_has[1 + q], yhas[d]), sy_[3 * d + 1 + q].start)
        for d in range(2):
            when(zhas[d], sz_[3 * d + 1].start)
        for d in range(2):
            when(yhas[d], sy_[3 * d].start)
        for d in range(2):
            r0, piece = ((my, 0), (NY, 2))[d]
            for q in range(2):
                z0 = ZED[1 + q][0]

                def add(d=d, q=q, r0=r0, z0=z0):
                    sy_[3 * d + 1 + q].wait_recv()
                    c[r0:r0 + my, z0:z0 + HZ, :] += ry[d, :, z0:z0 + HZ, :]
                when(both(zed_has[1 + q], yfrom[d]), add)
                when(zed_has[1 + q], sz_[3 * (1 - q) + piece].start)
        for d in range(2):
            r0 = (my, NY)[d]

            def add_y(d=d, r0=r0):
                sy_[3 * d].wait_recv()
                c[r0:r0 + my, HZ:HZ + NH, :] += ry[d, :, HZ:HZ + NH, :]
            when(yfrom[d], add_y)
        for d in range(2):
            z0 = (HZ, NH)[d]

            def add_z(d=d, z0=z0):
                for p in range(3):
                    sz_[3 * d + p].wait_recv()
                c[my:my + NY, z0:z0 + HZ, :] += rz[d]
            when(zfrom[d], add_z)
        for d in range(2):
            for p in range(3):
                when(zhas[d], sz_[3 * d + p].wait_send)
            when(yhas[d], sy_[3 * d].wait_send)
            for q in range(2):
                when(both(zed_has[1 + q], yhas[d]), sy_[3 * d + 1 + q].wait_send)

    gather_begin(0)
    swap_prof = pltpu.make_async_remote_copy(
        src_ref=mine, dst_ref=theirs, send_sem=xssem.at[0], recv_sem=xrsem.at[0],
        device_id=partner, device_id_type=MESH)
    swap_prof.start()
    swap_obs = pltpu.make_async_remote_copy(
        src_ref=obs_hbm.at[0, pl.ds((1 - v) * NH, NH)], dst_ref=obs_z.at[v],
        send_sem=xssem.at[1], recv_sem=xrsem.at[1], device_id=partner, device_id_type=MESH)
    swap_obs.start()

    swap_prof.wait()
    own, other = mine[...], theirs[...]
    prof = (jnp.where(v == 0, own, other), jnp.where(v == 0, other, own))

    def tap(view, row, a):
        return prof[view][row:row + 1, a:a + 1]

    rows = lax.broadcasted_iota(jnp.int32, (NE, 3 * NE), 0)
    cols = lax.broadcasted_iota(jnp.int32, (NE, 3 * NE), 1)
    third = cols // NE
    cols = cols - third * NE

    def banded(diff, view, row, taps):
        w = jnp.zeros(diff.shape, F32)
        for a in range(taps):
            w = jnp.where(diff == a, tap(view, row, a), w)
        return w

    off = HZ - mz
    for ref, inner, outer in ((wf, rows, cols), (wb, cols, rows)):
        second = inner >= NH
        diff = outer - jnp.where(second, inner - NH, inner) - off
        w = jnp.where(second, banded(diff, 1, 0, KZ), banded(diff, 0, 0, KZ))
        high, low = split(w)
        ref[...] = jnp.where(third == 2, low.astype(F32), high.astype(F32)).astype(BF16)
    for view in range(2):
        for back in range(2):
            for r0 in range(0, NX, 64):
                r = lax.broadcasted_iota(jnp.int32, (64, NX), 0) + r0
                c = lax.broadcasted_iota(jnp.int32, (64, NX), 1)
                diff = (c - r if back else r - c) + mx
                high, low = split(banded(diff, view, 2, KX))
                tx[view, back, 0, r0:r0 + 64, :] = high
                tx[view, back, 1, r0:r0 + 64, :] = low
    wy = [[jnp.broadcast_to(tap(view, 1, b), (NH, NX)) for b in range(KY)] for view in range(2)]

    qbuf[0:2 * my] = jnp.zeros((2 * my, NE, NX), F32)
    qbuf[2 * my + NY:] = jnp.zeros((2 * my, NE, NX), F32)

    load_obs.wait()
    swap_obs.wait()
    for view in range(2):
        obs_t[view] = jnp.transpose(obs_z[view], (1, 0, 2))

    CH = 8

    def xblur(view, back):
        high, low = ybuf[0], ybuf[1]
        both_ = jnp.concatenate([high, low], axis=0)
        n = high.shape[0]
        d = jnp.dot(both_, tx[view, back, 0], preferred_element_type=F32)
        d2 = jnp.dot(high, tx[view, back, 1], preferred_element_type=F32)
        return d[:n] + (d[n:] + d2)

    def stacked(x):
        high, low = split(x)
        return jnp.concatenate([high, low, high], axis=0)

    for it in range(ITERS):
        gather_end(it)

        def zrow(y, carry):
            zbuf[y] = jnp.dot(wf[...], stacked(ebuf[it, y]), preferred_element_type=F32)
            return carry
        lax.fori_loop(0, NR, zrow, 0)

        for y0 in range(0, NY, CH):
            for view in range(2):
                z0 = view * NH
                for y in range(CH):
                    acc = wy[view][0] * zbuf[y0 + y, z0:z0 + NH, :]
                    for b in range(1, KY):
                        acc = acc + wy[view][b] * zbuf[y0 + y + b, z0:z0 + NH, :]
                    high, low = split(acc)
                    ybuf[0, y * NH:(y + 1) * NH, :] = high
                    ybuf[1, y * NH:(y + 1) * NH, :] = low
                blurred = xblur(view, 0)
                quotient = obs_t[view, y0:y0 + CH].reshape(CH * NH, NX) / blurred
                high, low = split(quotient)
                ybuf[0] = high
                ybuf[1] = low
                qbuf[2 * my + y0:2 * my + y0 + CH, z0:z0 + NH, :] = xblur(view, 1).reshape(CH, NH, NX)

        def crow(r, carry):
            parts = []
            for view in range(2):
                z0 = view * NH
                acc = wy[view][0] * qbuf[r + 2 * my, z0:z0 + NH, :]
                for b in range(1, KY):
                    acc = acc + wy[view][b] * qbuf[r + 2 * my - b, z0:z0 + NH, :]
                parts.append(acc)
            cbuf[it, r] = jnp.dot(wb[...], stacked(jnp.concatenate(parts, axis=0)),
                                  preferred_element_type=F32)
            return carry
        lax.fori_loop(0, NR, crow, 0)

        scatter(it)
        new = ebuf[it, my:my + NY, HZ:HZ + NH, :] * (0.5 * cbuf[it, my:my + NY, HZ:HZ + NH, :])
        if it + 1 < ITERS:
            ebuf[it + 1, my:my + NY, HZ:HZ + NH, :] = new
            gather_begin(it + 1)
        else:
            stage[1] = jnp.transpose(new, (1, 0, 2))
            save = pltpu.make_async_copy(stage.at[1], out_hbm.at[pl.ds(v * NH, NH)], lsem.at[2])
            save.start()
            share = pltpu.make_async_remote_copy(
                src_ref=stage.at[1], dst_ref=out_hbm.at[pl.ds(v * NH, NH)],
                send_sem=xssem.at[2], recv_sem=xrsem.at[2], device_id=partner, device_id_type=MESH)
            share.start()
            save.wait()
            share.wait()


def on_device(S, G, observed, start, spread_z, spread_y, spread_x):
    NZ, NY, NX = start.shape
    KZ, KY, KX = spread_z.shape[1], spread_y.shape[1], spread_x.shape[1]
    NH = NZ // 2
    my = KY // 2
    HZ = -(-(KZ // 2) // 8) * 8
    NE, NR = NH + 2 * HZ, NY + 2 * my
    dims = (NH, NY, NX, HZ, KZ, KY, KX, S, G)
    vm = pltpu.VMEM
    anyspec = pl.BlockSpec(memory_space=pl.ANY)
    vspec = pl.BlockSpec(memory_space=pltpu.VMEM)
    return pl.pallas_call(
        functools.partial(kernel, dims),
        out_shape=jax.ShapeDtypeStruct((NZ, NY, NX), F32),
        in_specs=[anyspec, anyspec, vspec, vspec, vspec],
        out_specs=anyspec,
        scratch_shapes=[
            vm((2, NH, NY, NX), F32), vm((2, NH, NY, NX), F32), vm((2, NY, NH, NX), F32),
            vm((8, 128), F32), vm((8, 128), F32),
            vm((NE, 3 * NE), BF16), vm((NE, 3 * NE), BF16), vm((2, 2, 2, NX, NX), BF16),
            vm((NR, NE, NX), F32), vm((2, 8 * NH, NX), BF16), vm((NY + 4 * my, NE, NX), F32),
            vm((ITERS, NR, NE, NX), F32), vm((ITERS, NR, NE, NX), F32),
            vm((ITERS, 2, my, NE, NX), F32), vm((ITERS, 2, NY, HZ, NX), F32),
            pltpu.SemaphoreType.DMA((3,)),
            pltpu.SemaphoreType.DMA((2 * ITERS, 12)), pltpu.SemaphoreType.DMA((2 * ITERS, 12)),
            pltpu.SemaphoreType.DMA((3,)), pltpu.SemaphoreType.DMA((3,)),
        ],
        compiler_params=pltpu.CompilerParams(
            collective_id=0, has_side_effects=True, vmem_limit_bytes=48 << 20),
    )(observed, start, spread_z, spread_y, spread_x)


def solution(mesh):
    S, G = 2 * mesh.shape["gz"], mesh.shape["gy"]
    return jax.shard_map(
        functools.partial(on_device, S, G),
        mesh=mesh,
        in_specs=(
            P("view", "gz", "gy", None),
            P("gz", "gy", None),
            P("view", None),
            P("view", None),
            P("view", None),
        ),
        out_specs=P("gz", "gy", None),
        check_vma=False,
    )
```

```python
import functools

import jax
import jax.numpy as jnp
from jax import lax
from jax.experimental import pallas as pl
from jax.experimental.pallas import tpu as pltpu
from jax.sharding import PartitionSpec as P

ITERS = 2
MESH = pl.DeviceIdType.MESH
F32 = jnp.float32
BF16 = jnp.bfloat16


def split(x):
    high = x.astype(BF16)
    return high, (x - high.astype(F32)).astype(BF16)


def kernel(dims, obs_hbm, start_hbm, sz_ref, sy_ref, sx_ref, out_hbm,
           raw_z, raw_y, raw_x, stage, obs_z, obs_t, mine, theirs, wf, wb, tx, zbuf, ybuf, qbuf,
           ebuf, cbuf, rybuf, rzbuf, lsem, ssem, rsem, xssem, xrsem):
    NH, NY, NX, HZ, KZ, KY, KX, S, G = dims
    my, mz, mx = KY // 2, KZ // 2, KX // 2
    NE, NR = NH + 2 * HZ, NY + 2 * my
    v = lax.axis_index("view")
    gy = lax.axis_index("gy")
    s = 2 * lax.axis_index("gz") + v
    up_z, dn_z = s < S - 1, s > 0
    up_y, dn_y = gy < G - 1, gy > 0

    def zdev(t):
        t = lax.rem(t + S, S)
        return {"view": lax.rem(t, 2), "gz": t // 2}

    def ydev(t):
        return {"gy": lax.rem(t + G, G)}

    zto = (zdev(s + 1), zdev(s - 1))
    yto = (ydev(gy + 1), ydev(gy - 1))
    partner = {"view": 1 - v}
    zhas, yhas = (up_z, dn_z), (up_y, dn_y)
    zfrom, yfrom = (dn_z, up_z), (dn_y, up_y)

    load_start = pltpu.make_async_copy(start_hbm.at[pl.ds(v * NH, NH)], stage.at[0], lsem.at[0])
    load_start.start()
    load_obs = pltpu.make_async_copy(obs_hbm.at[0, pl.ds(v * NH, NH)], obs_z.at[v], lsem.at[1])
    load_obs.start()
    loads = [pltpu.make_async_copy(ref, raw, lsem.at[3 + row])
             for row, (ref, raw) in enumerate(((sz_ref, raw_z), (sy_ref, raw_y), (sx_ref, raw_x)))]
    for load in loads:
        load.start()

    barrier = pltpu.get_barrier_semaphore()
    for has, to in ((up_z, zto[0]), (dn_z, zto[1]), (up_y, yto[0]), (dn_y, yto[1])):
        @pl.when(has)
        def _(to=to):
            pl.semaphore_signal(barrier, inc=1, device_id=to, device_id_type=MESH)

    for it in range(ITERS):
        for d in range(2):
            @pl.when(jnp.logical_not(zfrom[d]))
            def _(it=it, d=d):
                z0 = (0, HZ + NH)[d]
                ebuf[it, :, z0:z0 + HZ, :] = jnp.zeros((NR, HZ, NX), F32)

            @pl.when(jnp.logical_not(yfrom[d]))
            def _(it=it, d=d):
                r0 = (0, my + NY)[d]
                ebuf[it, r0:r0 + my] = jnp.zeros((my, NE, NX), F32)

    load_start.wait()
    ebuf[0, my:my + NY, HZ:HZ + NH, :] = jnp.transpose(stage[0], (1, 0, 2))

    peers = sum(has.astype(jnp.int32) for has in (up_z, dn_z, up_y, dn_y))
    pl.semaphore_wait(barrier, peers)

    def copy(phase, m, src, dst, to):
        return pltpu.make_async_remote_copy(
            src_ref=src, dst_ref=dst, send_sem=ssem.at[phase, m], recv_sem=rsem.at[phase, m],
            device_id=to, device_id_type=MESH)

    half = (NY - 2 * my) // 2
    ROWS = ((my, my), (NY, my), (2 * my, half), (2 * my + half, NY - 2 * my - half))
    ZED = ((HZ, NH), (0, HZ), (HZ + NH, HZ))
    ENDS, MID = (0, 1), (2, 3)

    def when(cond, fn):
        @pl.when(cond)
        def _():
            fn()

    def both(a, b):
        return jnp.logical_and(a, b)

    zed_has = (None, dn_z, up_z)

    def gz(it, d, p):
        e = ebuf.at[it]
        src0, dst0 = ((NH, 0), (HZ, HZ + NH))[d]
        r0, n = ROWS[p]
        return copy(2 * it, 4 * d + p, e.at[pl.ds(r0, n), pl.ds(src0, HZ)],
                    e.at[pl.ds(r0, n), pl.ds(dst0, HZ)], zto[d])

    def gyc(it, d, p):
        e = ebuf.at[it]
        src0, dst0 = ((NY, 0), (my, my + NY))[d]
        z0, n = ZED[p]
        return copy(2 * it, 8 + 3 * d + p, e.at[pl.ds(src0, my), pl.ds(z0, n)],
                    e.at[pl.ds(dst0, my), pl.ds(z0, n)], yto[d])

    def sz(it, d, p):
        src0 = (HZ + NH, 0)[d]
        r0, n = ROWS[p]
        return copy(2 * it + 1, 4 * d + p, cbuf.at[it, pl.ds(r0, n), pl.ds(src0, HZ)],
                    rzbuf.at[it, d, pl.ds(r0 - my, n)], zto[d])

    def sy(it, d, p):
        src0 = (my + NY, 0)[d]
        z0, n = ZED[p]
        return copy(2 * it + 1, 8 + 3 * d + p, cbuf.at[it, pl.ds(src0, my), pl.ds(z0, n)],
                    rybuf.at[it, d, :, pl.ds(z0, n)], yto[d])

    def gather_piece(it, p):
        for d in range(2):
            when(zhas[d], gz(it, d, p).start)

    def gather_own(it):
        for d in range(2):
            when(yhas[d], gyc(it, d, 0).start)

    def gather_take(it, p):
        for d in range(2):
            when(zfrom[d], gz(it, d, p).wait_recv)
            if p in ENDS:
                dy = 1 - p
                when(both(zfrom[d], yhas[dy]), gyc(it, dy, 1 + d).start)

    def gather_edge(it, d):
        when(yfrom[d], gyc(it, d, 0).wait_recv)
        for q in range(2):
            when(both(zed_has[1 + q], yfrom[d]), gyc(it, d, 1 + q).wait_recv)

    def sent(it, z, y):
        for d in range(2):
            for p in range(4):
                when(zhas[d], z(it, d, p).wait_send)
            when(yhas[d], y(it, d, 0).wait_send)
            for q in range(2):
                when(both(zed_has[1 + q], yhas[d]), y(it, d, 1 + q).wait_send)

    def scatter_edges(it):
        for q in range(2):
            for d in range(2):
                when(both(zed_has[1 + q], yhas[d]), sy(it, d, 1 + q).start)
        for d in range(2):
            when(yhas[d], sy(it, d, 0).start)

    def scatter_piece(it, p):
        for d in range(2):
            when(zhas[d], sz(it, d, p).start)

    def scatter_end(it, p):
        d, r0 = p, ROWS[p][0]
        for q in range(2):
            z0 = ZED[1 + q][0]

            def add(q=q, z0=z0):
                sy(it, d, 1 + q).wait_recv()
                cbuf[it, r0:r0 + my, z0:z0 + HZ, :] += rybuf[it, d, :, z0:z0 + HZ, :]
            when(both(zed_has[1 + q], yfrom[d]), add)
            when(zed_has[1 + q], sz(it, 1 - q, p).start)

    def scatter_take(it, p):
        r0, n = ROWS[p]
        if p in ENDS:
            def add_y():
                sy(it, p, 0).wait_recv()
                cbuf[it, r0:r0 + n, HZ:HZ + NH, :] += rybuf[it, p, :, HZ:HZ + NH, :]
            when(yfrom[p], add_y)
        for d in range(2):
            z0 = (HZ, NH)[d]

            def add_z(d=d, z0=z0):
                sz(it, d, p).wait_recv()
                cbuf[it, r0:r0 + n, z0:z0 + HZ, :] += rzbuf[it, d, r0 - my:r0 - my + n]
            when(zfrom[d], add_z)

    for p in (0, 1, 2, 3):
        gather_piece(0, p)
    gather_own(0)
    mine[...] = jnp.zeros_like(mine)
    for row, (raw, taps) in enumerate(((raw_z, KZ), (raw_y, KY), (raw_x, KX))):
        loads[row].wait()
        mine[row:row + 1, 0:taps] = raw[...] / jnp.sum(raw[...], axis=1, keepdims=True)
    swap_prof = pltpu.make_async_remote_copy(
        src_ref=mine, dst_ref=theirs, send_sem=xssem.at[0], recv_sem=xrsem.at[0],
        device_id=partner, device_id_type=MESH)
    swap_prof.start()
    swap_obs = pltpu.make_async_remote_copy(
        src_ref=obs_hbm.at[0, pl.ds((1 - v) * NH, NH)], dst_ref=obs_z.at[v],
        send_sem=xssem.at[1], recv_sem=xrsem.at[1], device_id=partner, device_id_type=MESH)
    swap_obs.start()

    swap_prof.wait()
    own, other = mine[...], theirs[...]
    prof = (jnp.where(v == 0, own, other), jnp.where(v == 0, other, own))

    def tap(view, row, a):
        return prof[view][row:row + 1, a:a + 1]

    rows = lax.broadcasted_iota(jnp.int32, (NE, 3 * NE), 0)
    cols = lax.broadcasted_iota(jnp.int32, (NE, 3 * NE), 1)
    third = cols // NE
    cols = cols - third * NE

    def banded(diff, view, row, taps):
        w = jnp.zeros(diff.shape, F32)
        for a in range(taps):
            w = jnp.where(diff == a, tap(view, row, a), w)
        return w

    off = HZ - mz
    for ref, inner, outer in ((wf, rows, cols), (wb, cols, rows)):
        second = inner >= NH
        diff = outer - jnp.where(second, inner - NH, inner) - off
        w = jnp.where(second, banded(diff, 1, 0, KZ), banded(diff, 0, 0, KZ))
        high, low = split(w)
        ref[...] = jnp.where(third == 2, low.astype(F32), high.astype(F32)).astype(BF16)
    for view in range(2):
        for back in range(2):
            for r0 in range(0, NX, 64):
                r = lax.broadcasted_iota(jnp.int32, (64, NX), 0) + r0
                c = lax.broadcasted_iota(jnp.int32, (64, NX), 1)
                diff = (c - r if back else r - c) + mx
                high, low = split(banded(diff, view, 2, KX))
                tx[view, back, 0, r0:r0 + 64, :] = high
                tx[view, back, 1, r0:r0 + 64, :] = low
    wy = [[jnp.broadcast_to(tap(view, 1, b), (NH, NX)) for b in range(KY)] for view in range(2)]

    qbuf[0:2 * my] = jnp.zeros((2 * my, NE, NX), F32)
    qbuf[2 * my + NY:] = jnp.zeros((2 * my, NE, NX), F32)

    load_obs.wait()
    swap_obs.wait()
    for view in range(2):
        obs_t[view] = jnp.transpose(obs_z[view], (1, 0, 2))

    CH = 8

    def xblur(view, back):
        high, low = ybuf[0], ybuf[1]
        both_ = jnp.concatenate([high, low], axis=0)
        n = high.shape[0]
        d = jnp.dot(both_, tx[view, back, 0], preferred_element_type=F32)
        d2 = jnp.dot(high, tx[view, back, 1], preferred_element_type=F32)
        return d[:n] + (d[n:] + d2)

    def stacked(x):
        high, low = split(x)
        return jnp.concatenate([high, low, high], axis=0)

    for it in range(ITERS):
        def zrow(y, carry, it=it):
            zbuf[y] = jnp.dot(wf[...], stacked(ebuf[it, y]), preferred_element_type=F32)
            return carry

        def zrows(r0, n):
            lax.fori_loop(r0, r0 + n, zrow, 0, unroll=True)

        for p in ((0, 1, 2, 3) if it == 0 else (2, 0, 1, 3)):
            gather_take(it, p)
            zrows(*ROWS[p])
        for d in range(2):
            gather_edge(it, d)
            zrows((0, my + NY)[d], my)

        for y0 in range(0, NY, CH):
            for view in range(2):
                z0 = view * NH
                for y in range(CH):
                    acc = wy[view][0] * zbuf[y0 + y, z0:z0 + NH, :]
                    for b in range(1, KY):
                        acc = acc + wy[view][b] * zbuf[y0 + y + b, z0:z0 + NH, :]
                    high, low = split(acc)
                    ybuf[0, y * NH:(y + 1) * NH, :] = high
                    ybuf[1, y * NH:(y + 1) * NH, :] = low
                blurred = xblur(view, 0)
                quotient = obs_t[view, y0:y0 + CH].reshape(CH * NH, NX) / blurred
                high, low = split(quotient)
                ybuf[0] = high
                ybuf[1] = low
                qbuf[2 * my + y0:2 * my + y0 + CH, z0:z0 + NH, :] = xblur(view, 1).reshape(CH, NH, NX)

        def crow(r, carry, it=it):
            parts = []
            for view in range(2):
                z0 = view * NH
                acc = wy[view][0] * qbuf[r + 2 * my, z0:z0 + NH, :]
                for b in range(1, KY):
                    acc = acc + wy[view][b] * qbuf[r + 2 * my - b, z0:z0 + NH, :]
                parts.append(acc)
            cbuf[it, r] = jnp.dot(wb[...], stacked(jnp.concatenate(parts, axis=0)),
                                  preferred_element_type=F32)
            return carry
        def crows(r0, n):
            lax.fori_loop(r0, r0 + n, crow, 0, unroll=True)

        crows(0, my)
        crows(my + NY, my)
        scatter_edges(it)
        for p in MID:
            crows(*ROWS[p])
            scatter_piece(it, p)
        for p in ENDS:
            crows(*ROWS[p])
        for p in ENDS:
            scatter_end(it, p)

        def update(p, it=it):
            r0, n = ROWS[p]
            scatter_take(it, p)
            new = ebuf[it, r0:r0 + n, HZ:HZ + NH, :] * (0.5 * cbuf[it, r0:r0 + n, HZ:HZ + NH, :])
            if it + 1 < ITERS:
                ebuf[it + 1, r0:r0 + n, HZ:HZ + NH, :] = new
            else:
                zbuf[r0:r0 + n, 0:NH, :] = new

        if it + 1 < ITERS:
            update(2)
            gather_piece(it + 1, 2)
            update(3)
            update(0)
            gather_piece(it + 1, 0)
            update(1)
            gather_piece(it + 1, 1)
            gather_own(it + 1)
            gather_piece(it + 1, 3)
        else:
            for p in (2, 3, 0, 1):
                update(p)
            stage[1] = jnp.transpose(zbuf[my:my + NY, 0:NH, :], (1, 0, 2))
            save = pltpu.make_async_copy(stage.at[1], out_hbm.at[pl.ds(v * NH, NH)], lsem.at[2])
            save.start()
            share = pltpu.make_async_remote_copy(
                src_ref=stage.at[1], dst_ref=out_hbm.at[pl.ds(v * NH, NH)],
                send_sem=xssem.at[2], recv_sem=xrsem.at[2], device_id=partner, device_id_type=MESH)
            share.start()
            save.wait()
            share.wait()
    for it in range(ITERS):
        sent(it, gz, gyc)
        sent(it, sz, sy)


def on_device(S, G, observed, start, spread_z, spread_y, spread_x):
    NZ, NY, NX = start.shape
    KZ, KY, KX = spread_z.shape[1], spread_y.shape[1], spread_x.shape[1]
    NH = NZ // 2
    my = KY // 2
    HZ = -(-(KZ // 2) // 8) * 8
    NE, NR = NH + 2 * HZ, NY + 2 * my
    dims = (NH, NY, NX, HZ, KZ, KY, KX, S, G)
    vm = pltpu.VMEM
    hbm = pl.BlockSpec(memory_space=pltpu.HBM)
    return pl.pallas_call(
        functools.partial(kernel, dims),
        out_shape=jax.ShapeDtypeStruct((NZ, NY, NX), F32),
        in_specs=[hbm] * 5,
        out_specs=hbm,
        scratch_shapes=[
            vm((1, KZ), F32), vm((1, KY), F32), vm((1, KX), F32),
            vm((2, NH, NY, NX), F32), vm((2, NH, NY, NX), F32), vm((2, NY, NH, NX), F32),
            vm((8, 128), F32), vm((8, 128), F32),
            vm((NE, 3 * NE), BF16), vm((NE, 3 * NE), BF16), vm((2, 2, 2, NX, NX), BF16),
            vm((NR, NE, NX), F32), vm((2, 8 * NH, NX), BF16), vm((NY + 4 * my, NE, NX), F32),
            vm((ITERS, NR, NE, NX), F32), vm((ITERS, NR, NE, NX), F32),
            vm((ITERS, 2, my, NE, NX), F32), vm((ITERS, 2, NY, HZ, NX), F32),
            pltpu.SemaphoreType.DMA((6,)),
            pltpu.SemaphoreType.DMA((2 * ITERS, 14)), pltpu.SemaphoreType.DMA((2 * ITERS, 14)),
            pltpu.SemaphoreType.DMA((3,)), pltpu.SemaphoreType.DMA((3,)),
        ],
        compiler_params=pltpu.CompilerParams(
            collective_id=0, has_side_effects=True, vmem_limit_bytes=48 << 20),
    )(observed, start, spread_z, spread_y, spread_x)


def solution(mesh):
    S, G = 2 * mesh.shape["gz"], mesh.shape["gy"]
    return jax.shard_map(
        functools.partial(on_device, S, G),
        mesh=mesh,
        in_specs=(
            P("view", "gz", "gy", None),
            P("gz", "gy", None),
            P("view", None),
            P("view", None),
            P("view", None),
        ),
        out_specs=P("gz", "gy", None),
        check_vma=False,
    )
```

```python
import functools

import jax
import jax.numpy as jnp
from jax import lax
from jax.experimental import pallas as pl
from jax.experimental.pallas import tpu as pltpu
from jax.sharding import PartitionSpec as P

ITERS = 2
MESH = pl.DeviceIdType.MESH
F32 = jnp.float32
BF16 = jnp.bfloat16


def split(x):
    high = x.astype(BF16)
    return high, (x - high.astype(F32)).astype(BF16)


def kernel(dims, obs_hbm, start_hbm, sz_ref, sy_ref, sx_ref, out_hbm,
           raw_z, raw_y, raw_x, stage, obs_z, obs_t, mine, theirs, wf, wb, tx, zbuf, ybuf, qbuf,
           ebuf, cbuf, rybuf, rzbuf, lsem, osem, ssem, rsem, xssem, xrsem):
    NH, NY, NX, HZ, KZ, KY, KX, S, G = dims
    my, mz, mx = KY // 2, KZ // 2, KX // 2
    NE, NR = NH + 2 * HZ, NY + 2 * my
    v = lax.axis_index("view")
    gy = lax.axis_index("gy")
    s = 2 * lax.axis_index("gz") + v
    up_z, dn_z = s < S - 1, s > 0
    up_y, dn_y = gy < G - 1, gy > 0

    def zdev(t):
        t = lax.rem(t + S, S)
        return {"view": lax.rem(t, 2), "gz": t // 2}

    def ydev(t):
        return {"gy": lax.rem(t + G, G)}

    zto = (zdev(s + 1), zdev(s - 1))
    yto = (ydev(gy + 1), ydev(gy - 1))
    partner = {"view": 1 - v}
    zhas, yhas = (up_z, dn_z), (up_y, dn_y)
    zfrom, yfrom = (dn_z, up_z), (dn_y, up_y)

    load_start = pltpu.make_async_copy(start_hbm.at[pl.ds(v * NH, NH)], stage.at[0], lsem.at[0])
    load_start.start()
    load_obs = pltpu.make_async_copy(obs_hbm.at[0, pl.ds(v * NH, NH)], obs_z.at[v], lsem.at[1])
    load_obs.start()
    loads = [pltpu.make_async_copy(ref, raw, lsem.at[3 + row])
             for row, (ref, raw) in enumerate(((sz_ref, raw_z), (sy_ref, raw_y), (sx_ref, raw_x)))]
    for load in loads:
        load.start()

    barrier = pltpu.get_barrier_semaphore()
    for has, to in ((up_z, zto[0]), (dn_z, zto[1]), (up_y, yto[0]), (dn_y, yto[1])):
        @pl.when(has)
        def _(to=to):
            pl.semaphore_signal(barrier, inc=1, device_id=to, device_id_type=MESH)

    for it in range(ITERS):
        for d in range(2):
            @pl.when(jnp.logical_not(zfrom[d]))
            def _(it=it, d=d):
                z0 = (0, HZ + NH)[d]
                ebuf[it, :, z0:z0 + HZ, :] = jnp.zeros((NR, HZ, NX), F32)

            @pl.when(jnp.logical_not(yfrom[d]))
            def _(it=it, d=d):
                r0 = (0, my + NY)[d]
                ebuf[it, r0:r0 + my] = jnp.zeros((my, NE, NX), F32)

    load_start.wait()
    ebuf[0, my:my + NY, HZ:HZ + NH, :] = jnp.transpose(stage[0], (1, 0, 2))

    peers = sum(has.astype(jnp.int32) for has in (up_z, dn_z, up_y, dn_y))
    pl.semaphore_wait(barrier, peers)

    def copy(phase, m, src, dst, to):
        return pltpu.make_async_remote_copy(
            src_ref=src, dst_ref=dst, send_sem=ssem.at[phase, m], recv_sem=rsem.at[phase, m],
            device_id=to, device_id_type=MESH)

    CH = NY // 2
    ROWS = ((my, my), (NY, my), (2 * my, CH - 2 * my), (CH, 2 * my), (CH + 2 * my, NY - CH - 2 * my))
    NP = len(ROWS)
    ZED = ((HZ, NH), (0, HZ), (HZ + NH, HZ))
    ENDS = (0, 1)

    def when(cond, fn):
        @pl.when(cond)
        def _():
            fn()

    def both(a, b):
        return jnp.logical_and(a, b)

    zed_has = (None, dn_z, up_z)

    def gz(it, d, p):
        e = ebuf.at[it]
        src0, dst0 = ((NH, 0), (HZ, HZ + NH))[d]
        r0, n = ROWS[p]
        return copy(2 * it, NP * d + p, e.at[pl.ds(r0, n), pl.ds(src0, HZ)],
                    e.at[pl.ds(r0, n), pl.ds(dst0, HZ)], zto[d])

    def gyc(it, d, p):
        e = ebuf.at[it]
        src0, dst0 = ((NY, 0), (my, my + NY))[d]
        z0, n = ZED[p]
        return copy(2 * it, 2 * NP + 3 * d + p, e.at[pl.ds(src0, my), pl.ds(z0, n)],
                    e.at[pl.ds(dst0, my), pl.ds(z0, n)], yto[d])

    def sz(it, d, p):
        src0 = (HZ + NH, 0)[d]
        r0, n = ROWS[p]
        return copy(2 * it + 1, NP * d + p, cbuf.at[it, pl.ds(r0, n), pl.ds(src0, HZ)],
                    rzbuf.at[it, d, pl.ds(r0 - my, n)], zto[d])

    def sy(it, d, p):
        src0 = (my + NY, 0)[d]
        z0, n = ZED[p]
        return copy(2 * it + 1, 2 * NP + 3 * d + p, cbuf.at[it, pl.ds(src0, my), pl.ds(z0, n)],
                    rybuf.at[it, d, :, pl.ds(z0, n)], yto[d])

    def gather_piece(it, p):
        for d in range(2):
            when(zhas[d], gz(it, d, p).start)

    def gather_own(it):
        for d in range(2):
            when(yhas[d], gyc(it, d, 0).start)

    def gather_take(it, p):
        for d in range(2):
            when(zfrom[d], gz(it, d, p).wait_recv)
            if p in ENDS:
                dy = 1 - p
                when(both(zfrom[d], yhas[dy]), gyc(it, dy, 1 + d).start)

    def gather_edge(it, d):
        when(yfrom[d], gyc(it, d, 0).wait_recv)
        for q in range(2):
            when(both(zed_has[1 + q], yfrom[d]), gyc(it, d, 1 + q).wait_recv)

    def sent(it, z, y):
        for d in range(2):
            for p in range(NP):
                when(zhas[d], z(it, d, p).wait_send)
            when(yhas[d], y(it, d, 0).wait_send)
            for q in range(2):
                when(both(zed_has[1 + q], yhas[d]), y(it, d, 1 + q).wait_send)

    def scatter_edge(it, d):
        for q in range(2):
            when(both(zed_has[1 + q], yhas[d]), sy(it, d, 1 + q).start)
        when(yhas[d], sy(it, d, 0).start)

    def scatter_piece(it, p):
        for d in range(2):
            when(zhas[d], sz(it, d, p).start)

    def scatter_end(it, p):
        d, r0 = p, ROWS[p][0]
        for q in range(2):
            z0 = ZED[1 + q][0]

            def add(q=q, z0=z0):
                sy(it, d, 1 + q).wait_recv()
                cbuf[it, r0:r0 + my, z0:z0 + HZ, :] += rybuf[it, d, :, z0:z0 + HZ, :]
            when(both(zed_has[1 + q], yfrom[d]), add)
            when(zed_has[1 + q], sz(it, 1 - q, p).start)

    def scatter_take(it, p):
        r0, n = ROWS[p]
        if p in ENDS:
            def add_y():
                sy(it, p, 0).wait_recv()
                cbuf[it, r0:r0 + n, HZ:HZ + NH, :] += rybuf[it, p, :, HZ:HZ + NH, :]
            when(yfrom[p], add_y)
        for d in range(2):
            z0 = (HZ, NH)[d]

            def add_z(d=d, z0=z0):
                sz(it, d, p).wait_recv()
                cbuf[it, r0:r0 + n, z0:z0 + HZ, :] += rzbuf[it, d, r0 - my:r0 - my + n]
            when(zfrom[d], add_z)

    for p in range(NP):
        gather_piece(0, p)
    gather_own(0)
    mine[...] = jnp.zeros_like(mine)
    for row, (raw, taps) in enumerate(((raw_z, KZ), (raw_y, KY), (raw_x, KX))):
        loads[row].wait()
        mine[row:row + 1, 0:taps] = raw[...] / jnp.sum(raw[...], axis=1, keepdims=True)
    swap_prof = pltpu.make_async_remote_copy(
        src_ref=mine, dst_ref=theirs, send_sem=xssem.at[0], recv_sem=xrsem.at[0],
        device_id=partner, device_id_type=MESH)
    swap_prof.start()
    swap_obs = pltpu.make_async_remote_copy(
        src_ref=obs_hbm.at[0, pl.ds((1 - v) * NH, NH)], dst_ref=obs_z.at[v],
        send_sem=xssem.at[1], recv_sem=xrsem.at[1], device_id=partner, device_id_type=MESH)
    swap_obs.start()

    swap_prof.wait()
    own, other = mine[...], theirs[...]
    prof = (jnp.where(v == 0, own, other), jnp.where(v == 0, other, own))

    def tap(view, row, a):
        return prof[view][row:row + 1, a:a + 1]

    rows = lax.broadcasted_iota(jnp.int32, (NE, 3 * NE), 0)
    cols = lax.broadcasted_iota(jnp.int32, (NE, 3 * NE), 1)
    third = cols // NE
    cols = cols - third * NE

    def banded(diff, view, row, taps):
        w = jnp.zeros(diff.shape, F32)
        for a in range(taps):
            w = jnp.where(diff == a, tap(view, row, a), w)
        return w

    off = HZ - mz
    for ref, inner, outer in ((wf, rows, cols), (wb, cols, rows)):
        second = inner >= NH
        diff = outer - jnp.where(second, inner - NH, inner) - off
        w = jnp.where(second, banded(diff, 1, 0, KZ), banded(diff, 0, 0, KZ))
        high, low = split(w)
        ref[...] = jnp.where(third == 2, low.astype(F32), high.astype(F32)).astype(BF16)
    for view in range(2):
        for back in range(2):
            for r0 in range(0, NX, 64):
                r = lax.broadcasted_iota(jnp.int32, (64, NX), 0) + r0
                c = lax.broadcasted_iota(jnp.int32, (64, NX), 1)
                diff = (c - r if back else r - c) + mx
                high, low = split(banded(diff, view, 2, KX))
                tx[view, back, 0, r0:r0 + 64, :] = high
                tx[view, back, 1, r0:r0 + 64, :] = low
    wy = [[jnp.broadcast_to(tap(view, 1, b), (NH, NX)) for b in range(KY)] for view in range(2)]

    qbuf[0:2 * my] = jnp.zeros((2 * my, NE, NX), F32)
    qbuf[2 * my + NY:] = jnp.zeros((2 * my, NE, NX), F32)

    load_obs.wait()
    swap_obs.wait()
    for view in range(2):
        obs_t[view] = jnp.transpose(obs_z[view], (1, 0, 2))

    def xblur(view, back):
        high, low = ybuf[0], ybuf[1]
        both_ = jnp.concatenate([high, low], axis=0)
        n = high.shape[0]
        d = jnp.dot(both_, tx[view, back, 0], preferred_element_type=F32)
        d2 = jnp.dot(high, tx[view, back, 1], preferred_element_type=F32)
        return d[:n] + (d[n:] + d2)

    def stacked(x):
        high, low = split(x)
        return jnp.concatenate([high, low, high], axis=0)

    for it in range(ITERS):
        def zrow(y, carry, it=it):
            zbuf[y] = jnp.dot(wf[...], stacked(ebuf[it, y]), preferred_element_type=F32)
            return carry

        def zrows(r0, n):
            lax.fori_loop(r0, r0 + n, zrow, 0, unroll=True)

        def half(y0, it=it):
            for view in range(2):
                z0 = view * NH
                for y in range(CH):
                    acc = wy[view][0] * zbuf[y0 + y, z0:z0 + NH, :]
                    for b in range(1, KY):
                        acc = acc + wy[view][b] * zbuf[y0 + y + b, z0:z0 + NH, :]
                    high, low = split(acc)
                    ybuf[0, y * NH:(y + 1) * NH, :] = high
                    ybuf[1, y * NH:(y + 1) * NH, :] = low
                blurred = xblur(view, 0)
                quotient = obs_t[view, y0:y0 + CH].reshape(CH * NH, NX) / blurred
                high, low = split(quotient)
                ybuf[0] = high
                ybuf[1] = low
                qbuf[2 * my + y0:2 * my + y0 + CH, z0:z0 + NH, :] = xblur(view, 1).reshape(CH, NH, NX)

        def crow(r, carry, it=it):
            parts = []
            for view in range(2):
                z0 = view * NH
                acc = wy[view][0] * qbuf[r + 2 * my, z0:z0 + NH, :]
                for b in range(1, KY):
                    acc = acc + wy[view][b] * qbuf[r + 2 * my - b, z0:z0 + NH, :]
                parts.append(acc)
            cbuf[it, r] = jnp.dot(wb[...], stacked(jnp.concatenate(parts, axis=0)),
                                  preferred_element_type=F32)
            return carry
        def crows(r0, n):
            lax.fori_loop(r0, r0 + n, crow, 0, unroll=True)

        for p in ((0, 1, 2, 3) if it == 0 else (2, 0, 1, 3)):
            gather_take(it, p)
            zrows(*ROWS[p])
        gather_edge(it, 0)
        zrows(0, my)
        half(0)
        crows(0, my)
        scatter_edge(it, 1)
        crows(*ROWS[2])
        scatter_piece(it, 2)
        gather_take(it, 4)
        zrows(*ROWS[4])
        gather_edge(it, 1)
        zrows(my + NY, my)
        half(CH)
        crows(my + NY, my)
        scatter_edge(it, 0)
        for p in (3, 4):
            crows(*ROWS[p])
            scatter_piece(it, p)
        for p in ENDS:
            crows(*ROWS[p])
            scatter_end(it, p)

        def update(p, it=it):
            r0, n = ROWS[p]
            scatter_take(it, p)
            new = ebuf[it, r0:r0 + n, HZ:HZ + NH, :] * (0.5 * cbuf[it, r0:r0 + n, HZ:HZ + NH, :])
            if it + 1 < ITERS:
                ebuf[it + 1, r0:r0 + n, HZ:HZ + NH, :] = new
            else:
                zbuf[r0:r0 + n, 0:NH, :] = new

        if it + 1 < ITERS:
            update(2)
            gather_piece(it + 1, 2)
            update(3)
            update(4)
            update(0)
            gather_piece(it + 1, 0)
            update(1)
            gather_piece(it + 1, 1)
            gather_own(it + 1)
            gather_piece(it + 1, 3)
            gather_piece(it + 1, 4)
        else:
            outs = []
            for n, p in enumerate((2, 3, 4, 0, 1)):
                update(p)
                r0, rows_ = ROWS[p]
                src = zbuf.at[pl.ds(r0, rows_), pl.ds(0, NH)]
                dst = out_hbm.at[pl.ds(r0 - my, rows_), pl.ds(v * NH, NH)]
                outs.append(pltpu.make_async_copy(src, dst, osem.at[n]))
                outs.append(pltpu.make_async_remote_copy(
                    src_ref=src, dst_ref=dst, send_sem=xssem.at[2 + n], recv_sem=xrsem.at[2 + n],
                    device_id=partner, device_id_type=MESH))
                outs[-1].start()
                outs[-2].start()
            for out in outs:
                out.wait()
    for it in range(ITERS):
        sent(it, gz, gyc)
        sent(it, sz, sy)


def on_device(S, G, observed, start, spread_z, spread_y, spread_x):
    NZ, NY, NX = start.shape
    KZ, KY, KX = spread_z.shape[1], spread_y.shape[1], spread_x.shape[1]
    NH = NZ // 2
    my = KY // 2
    HZ = -(-(KZ // 2) // 8) * 8
    NE, NR = NH + 2 * HZ, NY + 2 * my
    dims = (NH, NY, NX, HZ, KZ, KY, KX, S, G)
    vm = pltpu.VMEM
    hbm = pl.BlockSpec(memory_space=pltpu.HBM)
    out = pl.pallas_call(
        functools.partial(kernel, dims),
        out_shape=jax.ShapeDtypeStruct((NY, NZ, NX), F32),
        in_specs=[hbm] * 5,
        out_specs=hbm,
        scratch_shapes=[
            vm((1, KZ), F32), vm((1, KY), F32), vm((1, KX), F32),
            vm((1, NH, NY, NX), F32), vm((2, NH, NY, NX), F32), vm((2, NY, NH, NX), F32),
            vm((8, 128), F32), vm((8, 128), F32),
            vm((NE, 3 * NE), BF16), vm((NE, 3 * NE), BF16), vm((2, 2, 2, NX, NX), BF16),
            vm((NR, NE, NX), F32), vm((2, NY // 2 * NH, NX), BF16), vm((NY + 4 * my, NE, NX), F32),
            vm((ITERS, NR, NE, NX), F32), vm((ITERS, NR, NE, NX), F32),
            vm((ITERS, 2, my, NE, NX), F32), vm((ITERS, 2, NY, HZ, NX), F32),
            pltpu.SemaphoreType.DMA((6,)), pltpu.SemaphoreType.DMA((5,)),
            pltpu.SemaphoreType.DMA((2 * ITERS, 16)), pltpu.SemaphoreType.DMA((2 * ITERS, 16)),
            pltpu.SemaphoreType.DMA((7,)), pltpu.SemaphoreType.DMA((7,)),
        ],
        compiler_params=pltpu.CompilerParams(
            collective_id=0, has_side_effects=True, vmem_limit_bytes=67043328),
    )(observed, start, spread_z, spread_y, spread_x)
    return jnp.transpose(out, (1, 0, 2))


def solution(mesh):
    S, G = 2 * mesh.shape["gz"], mesh.shape["gy"]
    return jax.shard_map(
        functools.partial(on_device, S, G),
        mesh=mesh,
        in_specs=(
            P("view", "gz", "gy", None),
            P("gz", "gy", None),
            P("view", None),
            P("view", None),
            P("view", None),
        ),
        out_specs=P("gz", "gy", None),
        check_vma=False,
    )
```

```python
import functools

import jax
import jax.numpy as jnp
from jax import lax
from jax.experimental import pallas as pl
from jax.experimental.pallas import tpu as pltpu
from jax.sharding import PartitionSpec as P

ITERS = 2
MESH = pl.DeviceIdType.MESH
F32 = jnp.float32
BF16 = jnp.bfloat16


def split(x):
    high = x.astype(BF16)
    return high, (x - high.astype(F32)).astype(BF16)


def kernel(dims, obs_hbm, start_hbm, sz_ref, sy_ref, sx_ref, out_hbm,
           raw_z, raw_y, raw_x, stage, obs_z, obs_t, mine, theirs, wf, wb, tx, zbuf, ybuf, qbuf,
           ebuf, cbuf, rybuf, rzbuf, lsem, osem, ssem, rsem, xssem, xrsem):
    NH, NY, NX, HZ, KZ, KY, KX, S, G = dims
    my, mz, mx = KY // 2, KZ // 2, KX // 2
    NE, NR = NH + 2 * HZ, NY + 2 * my
    v = lax.axis_index("view")
    gy = lax.axis_index("gy")
    s = 2 * lax.axis_index("gz") + v
    up_z, dn_z = s < S - 1, s > 0
    up_y, dn_y = gy < G - 1, gy > 0

    def zdev(t):
        t = lax.rem(t + S, S)
        return {"view": lax.rem(t, 2), "gz": t // 2}

    def ydev(t):
        return {"gy": lax.rem(t + G, G)}

    zto = (zdev(s + 1), zdev(s - 1))
    yto = (ydev(gy + 1), ydev(gy - 1))
    partner = {"view": 1 - v}
    zhas, yhas = (up_z, dn_z), (up_y, dn_y)
    zfrom, yfrom = (dn_z, up_z), (dn_y, up_y)

    load_start = pltpu.make_async_copy(start_hbm.at[pl.ds(v * NH, NH)], stage.at[0], lsem.at[0])
    load_start.start()
    load_obs = pltpu.make_async_copy(obs_hbm.at[0, pl.ds(v * NH, NH)], obs_z.at[v], lsem.at[1])
    load_obs.start()
    loads = [pltpu.make_async_copy(ref, raw, lsem.at[3 + row])
             for row, (ref, raw) in enumerate(((sz_ref, raw_z), (sy_ref, raw_y), (sx_ref, raw_x)))]
    for load in loads:
        load.start()

    barrier = pltpu.get_barrier_semaphore()
    for has, to in ((up_z, zto[0]), (dn_z, zto[1]), (up_y, yto[0]), (dn_y, yto[1])):
        @pl.when(has)
        def _(to=to):
            pl.semaphore_signal(barrier, inc=1, device_id=to, device_id_type=MESH)

    for it in range(ITERS):
        for d in range(2):
            @pl.when(jnp.logical_not(zfrom[d]))
            def _(it=it, d=d):
                z0 = (0, HZ + NH)[d]
                ebuf[it, :, z0:z0 + HZ, :] = jnp.zeros((NR, HZ, NX), F32)

            @pl.when(jnp.logical_not(yfrom[d]))
            def _(it=it, d=d):
                r0 = (0, my + NY)[d]
                ebuf[it, r0:r0 + my] = jnp.zeros((my, NE, NX), F32)

    load_start.wait()
    ebuf[0, my:my + NY, HZ:HZ + NH, :] = jnp.transpose(stage[0], (1, 0, 2))

    peers = sum(has.astype(jnp.int32) for has in (up_z, dn_z, up_y, dn_y))
    pl.semaphore_wait(barrier, peers)

    def copy(phase, m, src, dst, to):
        return pltpu.make_async_remote_copy(
            src_ref=src, dst_ref=dst, send_sem=ssem.at[phase, m], recv_sem=rsem.at[phase, m],
            device_id=to, device_id_type=MESH)

    CH = NY // 2
    ROWS = ((my, my), (NY, my), (2 * my, CH - 2 * my), (CH, 2 * my), (CH + 2 * my, NY - CH - 2 * my))
    NP = len(ROWS)
    ZED = ((HZ, NH), (0, HZ), (HZ + NH, HZ))
    ENDS = (0, 1)

    def when(cond, fn):
        @pl.when(cond)
        def _():
            fn()

    def both(a, b):
        return jnp.logical_and(a, b)

    zed_has = (None, dn_z, up_z)

    def gz(it, d, p):
        e = ebuf.at[it]
        src0, dst0 = ((NH, 0), (HZ, HZ + NH))[d]
        r0, n = ROWS[p]
        return copy(2 * it, NP * d + p, e.at[pl.ds(r0, n), pl.ds(src0, HZ)],
                    e.at[pl.ds(r0, n), pl.ds(dst0, HZ)], zto[d])

    def gyc(it, d, p):
        e = ebuf.at[it]
        src0, dst0 = ((NY, 0), (my, my + NY))[d]
        z0, n = ZED[p]
        return copy(2 * it, 2 * NP + 3 * d + p, e.at[pl.ds(src0, my), pl.ds(z0, n)],
                    e.at[pl.ds(dst0, my), pl.ds(z0, n)], yto[d])

    def sz(it, d, p):
        src0 = (HZ + NH, 0)[d]
        r0, n = ROWS[p]
        return copy(2 * it + 1, NP * d + p, cbuf.at[it, pl.ds(r0, n), pl.ds(src0, HZ)],
                    rzbuf.at[it, d, pl.ds(r0 - my, n)], zto[d])

    def sy(it, d, p):
        src0 = (my + NY, 0)[d]
        z0, n = ZED[p]
        return copy(2 * it + 1, 2 * NP + 3 * d + p, cbuf.at[it, pl.ds(src0, my), pl.ds(z0, n)],
                    rybuf.at[it, d, :, pl.ds(z0, n)], yto[d])

    def gather_piece(it, p):
        for d in range(2):
            when(zhas[d], gz(it, d, p).start)

    def gather_own(it):
        for d in range(2):
            when(yhas[d], gyc(it, d, 0).start)

    def gather_take(it, p):
        for d in range(2):
            when(zfrom[d], gz(it, d, p).wait_recv)
            if p in ENDS:
                dy = 1 - p
                when(both(zfrom[d], yhas[dy]), gyc(it, dy, 1 + d).start)

    def gather_edge(it, d):
        when(yfrom[d], gyc(it, d, 0).wait_recv)
        for q in range(2):
            when(both(zed_has[1 + q], yfrom[d]), gyc(it, d, 1 + q).wait_recv)

    def sent(it, z, y):
        for d in range(2):
            for p in range(NP):
                when(zhas[d], z(it, d, p).wait_send)
            when(yhas[d], y(it, d, 0).wait_send)
            for q in range(2):
                when(both(zed_has[1 + q], yhas[d]), y(it, d, 1 + q).wait_send)

    def scatter_edge(it, d):
        for q in range(2):
            when(both(zed_has[1 + q], yhas[d]), sy(it, d, 1 + q).start)
        when(yhas[d], sy(it, d, 0).start)

    def scatter_piece(it, p):
        for d in range(2):
            when(zhas[d], sz(it, d, p).start)

    def scatter_end(it, p):
        d, r0 = p, ROWS[p][0]
        for q in range(2):
            z0 = ZED[1 + q][0]

            def add(q=q, z0=z0):
                sy(it, d, 1 + q).wait_recv()
                cbuf[it, r0:r0 + my, z0:z0 + HZ, :] += rybuf[it, d, :, z0:z0 + HZ, :]
            when(both(zed_has[1 + q], yfrom[d]), add)
            when(zed_has[1 + q], sz(it, 1 - q, p).start)

    def scatter_take(it, p):
        r0, n = ROWS[p]
        if p in ENDS:
            def add_y():
                sy(it, p, 0).wait_recv()
                cbuf[it, r0:r0 + n, HZ:HZ + NH, :] += rybuf[it, p, :, HZ:HZ + NH, :]
            when(yfrom[p], add_y)
        for d in range(2):
            z0 = (HZ, NH)[d]

            def add_z(d=d, z0=z0):
                sz(it, d, p).wait_recv()
                cbuf[it, r0:r0 + n, z0:z0 + HZ, :] += rzbuf[it, d, r0 - my:r0 - my + n]
            when(zfrom[d], add_z)

    for p in range(NP):
        gather_piece(0, p)
    gather_own(0)
    mine[...] = jnp.zeros_like(mine)
    for row, (raw, taps) in enumerate(((raw_z, KZ), (raw_y, KY), (raw_x, KX))):
        loads[row].wait()
        mine[row:row + 1, 0:taps] = raw[...] / jnp.sum(raw[...], axis=1, keepdims=True)
    swap_prof = pltpu.make_async_remote_copy(
        src_ref=mine, dst_ref=theirs, send_sem=xssem.at[0], recv_sem=xrsem.at[0],
        device_id=partner, device_id_type=MESH)
    swap_prof.start()
    swap_obs = pltpu.make_async_remote_copy(
        src_ref=obs_hbm.at[0, pl.ds((1 - v) * NH, NH)], dst_ref=obs_z.at[v],
        send_sem=xssem.at[1], recv_sem=xrsem.at[1], device_id=partner, device_id_type=MESH)
    swap_obs.start()

    swap_prof.wait()
    own, other = mine[...], theirs[...]
    prof = (jnp.where(v == 0, own, other), jnp.where(v == 0, other, own))

    def tap(view, row, a):
        return prof[view][row:row + 1, a:a + 1]

    rows = lax.broadcasted_iota(jnp.int32, (NE, 3 * NE), 0)
    cols = lax.broadcasted_iota(jnp.int32, (NE, 3 * NE), 1)
    third = cols // NE
    cols = cols - third * NE

    def banded(diff, view, row, taps):
        w = jnp.zeros(diff.shape, F32)
        for a in range(taps):
            w = jnp.where(diff == a, tap(view, row, a), w)
        return w

    off = HZ - mz
    for ref, inner, outer in ((wf, rows, cols), (wb, cols, rows)):
        second = inner >= NH
        diff = outer - jnp.where(second, inner - NH, inner) - off
        w = jnp.where(second, banded(diff, 1, 0, KZ), banded(diff, 0, 0, KZ))
        high, low = split(w)
        ref[...] = jnp.where(third == 2, low.astype(F32), high.astype(F32)).astype(BF16)
    for view in range(2):
        for back in range(2):
            for r0 in range(0, NX, 64):
                r = lax.broadcasted_iota(jnp.int32, (64, NX), 0) + r0
                c = lax.broadcasted_iota(jnp.int32, (64, NX), 1)
                diff = (c - r if back else r - c) + mx
                high, low = split(banded(diff, view, 2, KX))
                tx[view, back, 0, r0:r0 + 64, :] = high
                tx[view, back, 1, r0:r0 + 64, :] = low
    wy = [[jnp.broadcast_to(tap(view, 1, b), (NH, NX)) for b in range(KY)] for view in range(2)]

    qbuf[0:2 * my] = jnp.zeros((2 * my, NE, NX), F32)
    qbuf[2 * my + NY:] = jnp.zeros((2 * my, NE, NX), F32)

    load_obs.wait()
    swap_obs.wait()
    for view in range(2):
        obs_t[view] = jnp.transpose(obs_z[view], (1, 0, 2))

    def xblur(view, back):
        high, low = ybuf[0], ybuf[1]
        both_ = jnp.concatenate([high, low], axis=0)
        n = high.shape[0]
        d = jnp.dot(both_, tx[view, back, 0], preferred_element_type=F32)
        d2 = jnp.dot(high, tx[view, back, 1], preferred_element_type=F32)
        return d[:n] + (d[n:] + d2)

    def stacked(x):
        high, low = split(x)
        return jnp.concatenate([high, low, high], axis=0)

    for it in range(ITERS):
        def zrow(y, carry, it=it):
            zbuf[y] = jnp.dot(wf[...], stacked(ebuf[it, y]), preferred_element_type=F32)
            return carry

        def zrows(r0, n):
            lax.fori_loop(r0, r0 + n, zrow, 0, unroll=True)

        def half(y0, it=it):
            for view in range(2):
                z0 = view * NH
                for y in range(CH):
                    acc = wy[view][0] * zbuf[y0 + y, z0:z0 + NH, :]
                    for b in range(1, KY):
                        acc = acc + wy[view][b] * zbuf[y0 + y + b, z0:z0 + NH, :]
                    high, low = split(acc)
                    ybuf[0, y * NH:(y + 1) * NH, :] = high
                    ybuf[1, y * NH:(y + 1) * NH, :] = low
                blurred = xblur(view, 0)
                quotient = obs_t[view, y0:y0 + CH].reshape(CH * NH, NX) / blurred
                high, low = split(quotient)
                ybuf[0] = high
                ybuf[1] = low
                qbuf[2 * my + y0:2 * my + y0 + CH, z0:z0 + NH, :] = xblur(view, 1).reshape(CH, NH, NX)

        def crow(r, carry, it=it):
            parts = []
            for view in range(2):
                z0 = view * NH
                acc = wy[view][0] * qbuf[r + 2 * my, z0:z0 + NH, :]
                for b in range(1, KY):
                    acc = acc + wy[view][b] * qbuf[r + 2 * my - b, z0:z0 + NH, :]
                parts.append(acc)
            cbuf[it, r] = jnp.dot(wb[...], stacked(jnp.concatenate(parts, axis=0)),
                                  preferred_element_type=F32)
            return carry
        def crows(r0, n):
            lax.fori_loop(r0, r0 + n, crow, 0, unroll=True)

        for p in ((0, 1, 2, 3) if it == 0 else (2, 0, 1, 3)):
            gather_take(it, p)
            zrows(*ROWS[p])
        gather_edge(it, 0)
        zrows(0, my)
        half(0)
        crows(0, my)
        scatter_edge(it, 1)
        crows(*ROWS[2])
        scatter_piece(it, 2)
        gather_take(it, 4)
        zrows(*ROWS[4])
        gather_edge(it, 1)
        zrows(my + NY, my)
        half(CH)
        crows(my + NY, my)
        scatter_edge(it, 0)
        for p in (3, 4):
            crows(*ROWS[p])
            scatter_piece(it, p)
        for p in ENDS:
            crows(*ROWS[p])
            scatter_end(it, p)

        def update(p, it=it):
            r0, n = ROWS[p]
            scatter_take(it, p)
            new = ebuf[it, r0:r0 + n, HZ:HZ + NH, :] * (0.5 * cbuf[it, r0:r0 + n, HZ:HZ + NH, :])
            if it + 1 < ITERS:
                ebuf[it + 1, r0:r0 + n, HZ:HZ + NH, :] = new
            else:
                zbuf[r0:r0 + n, 0:NH, :] = new

        if it + 1 < ITERS:
            update(2)
            gather_piece(it + 1, 2)
            update(3)
            update(4)
            update(0)
            gather_piece(it + 1, 0)
            update(1)
            gather_piece(it + 1, 1)
            gather_own(it + 1)
            gather_piece(it + 1, 3)
            gather_piece(it + 1, 4)
        else:
            outs = []
            for n, p in enumerate((2, 3, 4, 0, 1)):
                update(p)
                r0, rows_ = ROWS[p]
                src = zbuf.at[pl.ds(r0, rows_), pl.ds(0, NH)]
                dst = out_hbm.at[pl.ds(r0 - my, rows_), pl.ds(v * NH, NH)]
                outs.append(pltpu.make_async_copy(src, dst, osem.at[n]))
                outs.append(pltpu.make_async_remote_copy(
                    src_ref=src, dst_ref=dst, send_sem=xssem.at[2 + n], recv_sem=xrsem.at[2 + n],
                    device_id=partner, device_id_type=MESH))
                outs[-1].start()
                outs[-2].start()
            for out in outs:
                out.wait()
    for it in range(ITERS):
        sent(it, gz, gyc)
        sent(it, sz, sy)


def turn(x_ref, o_ref):
    o_ref[...] = jnp.transpose(x_ref[...], (1, 0, 2))


def on_device(S, G, observed, start, spread_z, spread_y, spread_x):
    NZ, NY, NX = start.shape
    KZ, KY, KX = spread_z.shape[1], spread_y.shape[1], spread_x.shape[1]
    NH = NZ // 2
    my = KY // 2
    HZ = -(-(KZ // 2) // 8) * 8
    NE, NR = NH + 2 * HZ, NY + 2 * my
    dims = (NH, NY, NX, HZ, KZ, KY, KX, S, G)
    vm = pltpu.VMEM
    hbm = pl.BlockSpec(memory_space=pltpu.HBM)
    out = pl.pallas_call(
        functools.partial(kernel, dims),
        out_shape=jax.ShapeDtypeStruct((NY, NZ, NX), F32),
        in_specs=[hbm] * 5,
        out_specs=hbm,
        scratch_shapes=[
            vm((1, KZ), F32), vm((1, KY), F32), vm((1, KX), F32),
            vm((1, NH, NY, NX), F32), vm((2, NH, NY, NX), F32), vm((2, NY, NH, NX), F32),
            vm((8, 128), F32), vm((8, 128), F32),
            vm((NE, 3 * NE), BF16), vm((NE, 3 * NE), BF16), vm((2, 2, 2, NX, NX), BF16),
            vm((NR, NE, NX), F32), vm((2, NY // 2 * NH, NX), BF16), vm((NY + 4 * my, NE, NX), F32),
            vm((ITERS, NR, NE, NX), F32), vm((ITERS, NR, NE, NX), F32),
            vm((ITERS, 2, my, NE, NX), F32), vm((ITERS, 2, NY, HZ, NX), F32),
            pltpu.SemaphoreType.DMA((6,)), pltpu.SemaphoreType.DMA((5,)),
            pltpu.SemaphoreType.DMA((2 * ITERS, 16)), pltpu.SemaphoreType.DMA((2 * ITERS, 16)),
            pltpu.SemaphoreType.DMA((7,)), pltpu.SemaphoreType.DMA((7,)),
        ],
        compiler_params=pltpu.CompilerParams(
            collective_id=0, has_side_effects=True, vmem_limit_bytes=67043328),
    )(observed, start, spread_z, spread_y, spread_x)
    block = NZ // 4
    return pl.pallas_call(
        turn,
        grid=(NZ // block,),
        out_shape=jax.ShapeDtypeStruct((NZ, NY, NX), F32),
        in_specs=[pl.BlockSpec((NY, block, NX), lambda i: (0, i, 0))],
        out_specs=pl.BlockSpec((block, NY, NX), lambda i: (i, 0, 0)),
    )(out)


def solution(mesh):
    S, G = 2 * mesh.shape["gz"], mesh.shape["gy"]
    return jax.shard_map(
        functools.partial(on_device, S, G),
        mesh=mesh,
        in_specs=(
            P("view", "gz", "gy", None),
            P("gz", "gy", None),
            P("view", None),
            P("view", None),
            P("view", None),
        ),
        out_specs=P("gz", "gy", None),
        check_vma=False,
    )
```

```python
import functools

import jax
import jax.numpy as jnp
from jax import lax
from jax.experimental import pallas as pl
from jax.experimental.pallas import tpu as pltpu
from jax.sharding import PartitionSpec as P

ITERS = 2
MESH = pl.DeviceIdType.MESH
F32 = jnp.float32
BF16 = jnp.bfloat16


def split(x):
    high = x.astype(BF16)
    return high, (x - high.astype(F32)).astype(BF16)


def kernel(dims, obs_hbm, start_hbm, sz_ref, sy_ref, sx_ref, out_hbm,
           raw_z, raw_y, raw_x, peer, stage, obs_z, obs_t, mine, theirs, wf, wb, tx, zbuf, ybuf, qbuf,
           ebuf, cbuf, rybuf, rzbuf, lsem, osem, ssem, rsem, xssem, xrsem):
    NH, NY, NX, HZ, KZ, KY, KX, S, G = dims
    my, mz, mx = KY // 2, KZ // 2, KX // 2
    NE, NR = NH + 2 * HZ, NY + 2 * my
    v = lax.axis_index("view")
    gy = lax.axis_index("gy")
    s = 2 * lax.axis_index("gz") + v
    up_z, dn_z = s < S - 1, s > 0
    up_y, dn_y = gy < G - 1, gy > 0

    def zdev(t):
        t = lax.rem(t + S, S)
        return {"view": lax.rem(t, 2), "gz": t // 2}

    def ydev(t):
        return {"gy": lax.rem(t + G, G)}

    zto = (zdev(s + 1), zdev(s - 1))
    yto = (ydev(gy + 1), ydev(gy - 1))
    partner = {"view": 1 - v}
    zhas, yhas = (up_z, dn_z), (up_y, dn_y)
    zfrom, yfrom = (dn_z, up_z), (dn_y, up_y)

    load_start = pltpu.make_async_copy(start_hbm.at[pl.ds(v * NH, NH)], stage.at[0], lsem.at[0])
    load_start.start()
    load_obs = pltpu.make_async_copy(obs_hbm.at[0, pl.ds(v * NH, NH)], obs_z.at[v], lsem.at[1])
    load_obs.start()
    loads = [pltpu.make_async_copy(ref, raw, lsem.at[3 + row])
             for row, (ref, raw) in enumerate(((sz_ref, raw_z), (sy_ref, raw_y), (sx_ref, raw_x)))]
    for load in loads:
        load.start()

    barrier = pltpu.get_barrier_semaphore()
    for has, to in ((up_z, zto[0]), (dn_z, zto[1]), (up_y, yto[0]), (dn_y, yto[1])):
        @pl.when(has)
        def _(to=to):
            pl.semaphore_signal(barrier, inc=1, device_id=to, device_id_type=MESH)

    for it in range(ITERS):
        for d in range(2):
            @pl.when(jnp.logical_not(zfrom[d]))
            def _(it=it, d=d):
                z0 = (0, HZ + NH)[d]
                ebuf[it, :, z0:z0 + HZ, :] = jnp.zeros((NR, HZ, NX), F32)

            @pl.when(jnp.logical_not(yfrom[d]))
            def _(it=it, d=d):
                r0 = (0, my + NY)[d]
                ebuf[it, r0:r0 + my] = jnp.zeros((my, NE, NX), F32)

    load_start.wait()
    ebuf[0, my:my + NY, HZ:HZ + NH, :] = jnp.transpose(stage[0], (1, 0, 2))

    peers = sum(has.astype(jnp.int32) for has in (up_z, dn_z, up_y, dn_y))
    pl.semaphore_wait(barrier, peers)

    def copy(phase, m, src, dst, to):
        return pltpu.make_async_remote_copy(
            src_ref=src, dst_ref=dst, send_sem=ssem.at[phase, m], recv_sem=rsem.at[phase, m],
            device_id=to, device_id_type=MESH)

    CH = NY // 2
    ROWS = ((my, my), (NY, my), (2 * my, CH - 2 * my), (CH, 2 * my), (CH + 2 * my, NY - CH - 2 * my))
    NP = len(ROWS)
    ZED = ((HZ, NH), (0, HZ), (HZ + NH, HZ))
    ENDS = (0, 1)

    def when(cond, fn):
        @pl.when(cond)
        def _():
            fn()

    def both(a, b):
        return jnp.logical_and(a, b)

    zed_has = (None, dn_z, up_z)

    def gz(it, d, p):
        e = ebuf.at[it]
        src0, dst0 = ((NH, 0), (HZ, HZ + NH))[d]
        r0, n = ROWS[p]
        return copy(2 * it, NP * d + p, e.at[pl.ds(r0, n), pl.ds(src0, HZ)],
                    e.at[pl.ds(r0, n), pl.ds(dst0, HZ)], zto[d])

    def gyc(it, d, p):
        e = ebuf.at[it]
        src0, dst0 = ((NY, 0), (my, my + NY))[d]
        z0, n = ZED[p]
        return copy(2 * it, 2 * NP + 3 * d + p, e.at[pl.ds(src0, my), pl.ds(z0, n)],
                    e.at[pl.ds(dst0, my), pl.ds(z0, n)], yto[d])

    def sz(it, d, p):
        src0 = (HZ + NH, 0)[d]
        r0, n = ROWS[p]
        return copy(2 * it + 1, NP * d + p, cbuf.at[it, pl.ds(r0, n), pl.ds(src0, HZ)],
                    rzbuf.at[it, d, pl.ds(r0 - my, n)], zto[d])

    def sy(it, d, p):
        src0 = (my + NY, 0)[d]
        z0, n = ZED[p]
        return copy(2 * it + 1, 2 * NP + 3 * d + p, cbuf.at[it, pl.ds(src0, my), pl.ds(z0, n)],
                    rybuf.at[it, d, :, pl.ds(z0, n)], yto[d])

    def gather_piece(it, p):
        for d in range(2):
            when(zhas[d], gz(it, d, p).start)

    def gather_own(it):
        for d in range(2):
            when(yhas[d], gyc(it, d, 0).start)

    def gather_take(it, p):
        for d in range(2):
            when(zfrom[d], gz(it, d, p).wait_recv)
            if p in ENDS:
                dy = 1 - p
                when(both(zfrom[d], yhas[dy]), gyc(it, dy, 1 + d).start)

    def gather_edge(it, d):
        when(yfrom[d], gyc(it, d, 0).wait_recv)
        for q in range(2):
            when(both(zed_has[1 + q], yfrom[d]), gyc(it, d, 1 + q).wait_recv)

    def sent(it, z, y):
        for d in range(2):
            for p in range(NP):
                when(zhas[d], z(it, d, p).wait_send)
            when(yhas[d], y(it, d, 0).wait_send)
            for q in range(2):
                when(both(zed_has[1 + q], yhas[d]), y(it, d, 1 + q).wait_send)

    def scatter_edge(it, d):
        for q in range(2):
            when(both(zed_has[1 + q], yhas[d]), sy(it, d, 1 + q).start)
        when(yhas[d], sy(it, d, 0).start)

    def scatter_piece(it, p):
        for d in range(2):
            when(zhas[d], sz(it, d, p).start)

    def scatter_end(it, p):
        d, r0 = p, ROWS[p][0]
        for q in range(2):
            z0 = ZED[1 + q][0]

            def add(q=q, z0=z0):
                sy(it, d, 1 + q).wait_recv()
                cbuf[it, r0:r0 + my, z0:z0 + HZ, :] += rybuf[it, d, :, z0:z0 + HZ, :]
            when(both(zed_has[1 + q], yfrom[d]), add)
            when(zed_has[1 + q], sz(it, 1 - q, p).start)

    def scatter_take(it, p):
        r0, n = ROWS[p]
        if p in ENDS:
            def add_y():
                sy(it, p, 0).wait_recv()
                cbuf[it, r0:r0 + n, HZ:HZ + NH, :] += rybuf[it, p, :, HZ:HZ + NH, :]
            when(yfrom[p], add_y)
        for d in range(2):
            z0 = (HZ, NH)[d]

            def add_z(d=d, z0=z0):
                sz(it, d, p).wait_recv()
                cbuf[it, r0:r0 + n, z0:z0 + HZ, :] += rzbuf[it, d, r0 - my:r0 - my + n]
            when(zfrom[d], add_z)

    for p in range(NP):
        gather_piece(0, p)
    gather_own(0)
    mine[...] = jnp.zeros_like(mine)
    for row, (raw, taps) in enumerate(((raw_z, KZ), (raw_y, KY), (raw_x, KX))):
        loads[row].wait()
        mine[row:row + 1, 0:taps] = raw[...] / jnp.sum(raw[...], axis=1, keepdims=True)
    swap_prof = pltpu.make_async_remote_copy(
        src_ref=mine, dst_ref=theirs, send_sem=xssem.at[0], recv_sem=xrsem.at[0],
        device_id=partner, device_id_type=MESH)
    swap_prof.start()
    swap_obs = pltpu.make_async_remote_copy(
        src_ref=obs_hbm.at[0, pl.ds((1 - v) * NH, NH)], dst_ref=obs_z.at[v],
        send_sem=xssem.at[1], recv_sem=xrsem.at[1], device_id=partner, device_id_type=MESH)
    swap_obs.start()

    swap_prof.wait()
    own, other = mine[...], theirs[...]
    prof = (jnp.where(v == 0, own, other), jnp.where(v == 0, other, own))

    def tap(view, row, a):
        return prof[view][row:row + 1, a:a + 1]

    rows = lax.broadcasted_iota(jnp.int32, (NE, 3 * NE), 0)
    cols = lax.broadcasted_iota(jnp.int32, (NE, 3 * NE), 1)
    third = cols // NE
    cols = cols - third * NE

    def banded(diff, view, row, taps):
        w = jnp.zeros(diff.shape, F32)
        for a in range(taps):
            w = jnp.where(diff == a, tap(view, row, a), w)
        return w

    off = HZ - mz
    for ref, inner, outer in ((wf, rows, cols), (wb, cols, rows)):
        second = inner >= NH
        diff = outer - jnp.where(second, inner - NH, inner) - off
        w = jnp.where(second, banded(diff, 1, 0, KZ), banded(diff, 0, 0, KZ))
        high, low = split(w)
        ref[...] = jnp.where(third == 2, low.astype(F32), high.astype(F32)).astype(BF16)
    for view in range(2):
        for back in range(2):
            for r0 in range(0, NX, 64):
                r = lax.broadcasted_iota(jnp.int32, (64, NX), 0) + r0
                c = lax.broadcasted_iota(jnp.int32, (64, NX), 1)
                diff = (c - r if back else r - c) + mx
                high, low = split(banded(diff, view, 2, KX))
                tx[view, back, 0, r0:r0 + 64, :] = high
                tx[view, back, 1, r0:r0 + 64, :] = low
    wy = [[jnp.broadcast_to(tap(view, 1, b), (NH, NX)) for b in range(KY)] for view in range(2)]

    qbuf[0:2 * my] = jnp.zeros((2 * my, NE, NX), F32)
    qbuf[2 * my + NY:] = jnp.zeros((2 * my, NE, NX), F32)

    load_obs.wait()
    swap_obs.wait()
    for view in range(2):
        obs_t[view] = jnp.transpose(obs_z[view], (1, 0, 2))

    def xblur(view, back):
        high, low = ybuf[0], ybuf[1]
        both_ = jnp.concatenate([high, low], axis=0)
        n = high.shape[0]
        d = jnp.dot(both_, tx[view, back, 0], preferred_element_type=F32)
        d2 = jnp.dot(high, tx[view, back, 1], preferred_element_type=F32)
        return d[:n] + (d[n:] + d2)

    def stacked(x):
        high, low = split(x)
        return jnp.concatenate([high, low, high], axis=0)

    for it in range(ITERS):
        def zrow(y, carry, it=it):
            zbuf[y] = jnp.dot(wf[...], stacked(ebuf[it, y]), preferred_element_type=F32)
            return carry

        def zrows(r0, n):
            lax.fori_loop(r0, r0 + n, zrow, 0, unroll=True)

        def half(y0, it=it):
            for view in range(2):
                z0 = view * NH
                for y in range(CH):
                    acc = wy[view][0] * zbuf[y0 + y, z0:z0 + NH, :]
                    for b in range(1, KY):
                        acc = acc + wy[view][b] * zbuf[y0 + y + b, z0:z0 + NH, :]
                    high, low = split(acc)
                    ybuf[0, y * NH:(y + 1) * NH, :] = high
                    ybuf[1, y * NH:(y + 1) * NH, :] = low
                blurred = xblur(view, 0)
                quotient = obs_t[view, y0:y0 + CH].reshape(CH * NH, NX) / blurred
                high, low = split(quotient)
                ybuf[0] = high
                ybuf[1] = low
                qbuf[2 * my + y0:2 * my + y0 + CH, z0:z0 + NH, :] = xblur(view, 1).reshape(CH, NH, NX)

        def crow(r, carry, it=it):
            parts = []
            for view in range(2):
                z0 = view * NH
                acc = wy[view][0] * qbuf[r + 2 * my, z0:z0 + NH, :]
                for b in range(1, KY):
                    acc = acc + wy[view][b] * qbuf[r + 2 * my - b, z0:z0 + NH, :]
                parts.append(acc)
            cbuf[it, r] = jnp.dot(wb[...], stacked(jnp.concatenate(parts, axis=0)),
                                  preferred_element_type=F32)
            return carry
        def crows(r0, n):
            lax.fori_loop(r0, r0 + n, crow, 0, unroll=True)

        for p in ((0, 1, 2, 3) if it == 0 else (2, 0, 1, 3)):
            gather_take(it, p)
            zrows(*ROWS[p])
        gather_edge(it, 0)
        zrows(0, my)
        half(0)
        crows(0, my)
        scatter_edge(it, 1)
        crows(*ROWS[2])
        scatter_piece(it, 2)
        gather_take(it, 4)
        zrows(*ROWS[4])
        gather_edge(it, 1)
        zrows(my + NY, my)
        half(CH)
        crows(my + NY, my)
        scatter_edge(it, 0)
        for p in (3, 4):
            crows(*ROWS[p])
            scatter_piece(it, p)
        for p in ENDS:
            crows(*ROWS[p])
            scatter_end(it, p)

        def update(p, it=it):
            r0, n = ROWS[p]
            scatter_take(it, p)
            new = ebuf[it, r0:r0 + n, HZ:HZ + NH, :] * (0.5 * cbuf[it, r0:r0 + n, HZ:HZ + NH, :])
            if it + 1 < ITERS:
                ebuf[it + 1, r0:r0 + n, HZ:HZ + NH, :] = new
            else:
                zbuf[r0:r0 + n, 0:NH, :] = new

        if it + 1 < ITERS:
            update(2)
            gather_piece(it + 1, 2)
            update(3)
            update(4)
            update(0)
            gather_piece(it + 1, 0)
            update(1)
            gather_piece(it + 1, 1)
            gather_own(it + 1)
            gather_piece(it + 1, 3)
            gather_piece(it + 1, 4)
        else:
            outs = []
            for n, p in enumerate((2, 3, 4, 0, 1)):
                update(p)
                r0, rows_ = ROWS[p]
                src = zbuf.at[pl.ds(r0, rows_), pl.ds(0, NH)]
                outs.append(pltpu.make_async_remote_copy(
                    src_ref=src, dst_ref=peer.at[pl.ds(r0 - my, rows_)],
                    send_sem=xssem.at[2 + n], recv_sem=xrsem.at[2 + n],
                    device_id=partner, device_id_type=MESH))
                outs[-1].start()
            stage[1] = jnp.transpose(zbuf[my:my + NY, 0:NH, :], (1, 0, 2))
            save = pltpu.make_async_copy(stage.at[1], out_hbm.at[pl.ds(v * NH, NH)], osem.at[0])
            save.start()
            for out in outs:
                out.wait()
            stage[2] = jnp.transpose(peer[...], (1, 0, 2))
            save2 = pltpu.make_async_copy(stage.at[2], out_hbm.at[pl.ds((1 - v) * NH, NH)], osem.at[1])
            save2.start()
            save.wait()
            save2.wait()
    for it in range(ITERS):
        sent(it, gz, gyc)
        sent(it, sz, sy)


def on_device(S, G, observed, start, spread_z, spread_y, spread_x):
    NZ, NY, NX = start.shape
    KZ, KY, KX = spread_z.shape[1], spread_y.shape[1], spread_x.shape[1]
    NH = NZ // 2
    my = KY // 2
    HZ = -(-(KZ // 2) // 8) * 8
    NE, NR = NH + 2 * HZ, NY + 2 * my
    dims = (NH, NY, NX, HZ, KZ, KY, KX, S, G)
    vm = pltpu.VMEM
    hbm = pl.BlockSpec(memory_space=pltpu.HBM)
    out = pl.pallas_call(
        functools.partial(kernel, dims),
        out_shape=jax.ShapeDtypeStruct((NZ, NY, NX), F32),
        in_specs=[hbm] * 5,
        out_specs=hbm,
        scratch_shapes=[
            vm((1, KZ), F32), vm((1, KY), F32), vm((1, KX), F32),
            vm((NY, NH, NX), F32), vm((3, NH, NY, NX), F32), vm((2, NH, NY, NX), F32), vm((2, NY, NH, NX), F32),
            vm((8, 128), F32), vm((8, 128), F32),
            vm((NE, 3 * NE), BF16), vm((NE, 3 * NE), BF16), vm((2, 2, 2, NX, NX), BF16),
            vm((NR, NE, NX), F32), vm((2, NY // 2 * NH, NX), BF16), vm((NY + 4 * my, NE, NX), F32),
            vm((ITERS, NR, NE, NX), F32), vm((ITERS, NR, NE, NX), F32),
            vm((ITERS, 2, my, NE, NX), F32), vm((ITERS, 2, NY, HZ, NX), F32),
            pltpu.SemaphoreType.DMA((6,)), pltpu.SemaphoreType.DMA((5,)),
            pltpu.SemaphoreType.DMA((2 * ITERS, 16)), pltpu.SemaphoreType.DMA((2 * ITERS, 16)),
            pltpu.SemaphoreType.DMA((7,)), pltpu.SemaphoreType.DMA((7,)),
        ],
        compiler_params=pltpu.CompilerParams(
            collective_id=0, has_side_effects=True, vmem_limit_bytes=67043328),
    )(observed, start, spread_z, spread_y, spread_x)
    return out


def solution(mesh):
    S, G = 2 * mesh.shape["gz"], mesh.shape["gy"]
    return jax.shard_map(
        functools.partial(on_device, S, G),
        mesh=mesh,
        in_specs=(
            P("view", "gz", "gy", None),
            P("gz", "gy", None),
            P("view", None),
            P("view", None),
            P("view", None),
        ),
        out_specs=P("gz", "gy", None),
        check_vma=False,
    )
```
